32 devices in a mesh: ctx: 8 (over y, x, core), chan: 4 (over z).
Axes of the slice: x: 2, y: 2, z: 4, core: 2. Of those that a mesh axis runs over, the one named last changes fastest.
Arguments:
- inputs: bfloat16 [256, 4096], P('ctx', 'chan'), may hold values from -6 to 6
- gain: float32 [4096], replicated, may hold values from 0.25 to 1.75
- w_in: bfloat16 [4096, 3, 4096], P(None, None, 'chan'), may hold values from -0.09375 to 0.09375
- w_out: bfloat16 [4096, 4096], P('chan'), may hold values from -0.125 to 0.125
- history: bfloat16 [2048, 2, 4096], P('ctx', None, 'chan'), may hold values from -6 to 6
- filt_far: bfloat16 [2048, 2, 4096], P('ctx', None, 'chan'), may hold values from -0.125 to 0.125
- filt_near: bfloat16 [256, 2, 4096], P(None, None, 'chan'), may hold values from -0.125 to 0.125
Outputs:
- mixed: bfloat16 [256, 4096], P('ctx', 'chan')
- gated: bfloat16 [256, 4096], P('ctx', 'chan')
The draws below stay inside these ranges and needn't reach their ends.
All inputs are finite; a program needn't handle non-finite values.
Results may differ from the reference program's by a relative error of at most 0.0066.
Values may be sent and summed in bfloat16 or wider, within the bound.
A program may use at most 128 MiB of HBM per device.

```python
import jax
import jax.numpy as jnp
from jax import lax

D = 4096
NEW = 256
H = 2048


def strengthened(drawn, key, source, target, parts, factor):
    owner, partner = [(jnp.arange(drawn.shape[position]) // (drawn.shape[position] // parts)).reshape([-1 if axis == position else 1 for axis in range(drawn.ndim)]) for position in (source, target)]
    chosen = jax.random.permutation(key, parts)[partner]
    strong = (owner == chosen) | (owner == (partner + parts // 2) % parts)
    return jnp.where(strong, factor * drawn, drawn)


def levels(stream_key, dims, pieces, smallest, largest):
    def one(dim, parts):
        steps = jax.random.uniform(jax.random.fold_in(jax.random.fold_in(stream_key, 6), dim), (parts,), jnp.float32, smallest / len(pieces), largest / len(pieces))
        return jnp.repeat(jnp.exp(steps), dims[dim] // parts).reshape((-1,) + (1,) * (len(dims) - dim - 1))

    factor_of = one(*pieces[0])
    for cut in pieces[1:]:
        factor_of = factor_of * one(*cut)
    return factor_of


def centred(own_key, extent, deviation, reach, pieces=(), kind=jnp.bfloat16):
    entries = jax.random.normal(own_key, extent, jnp.float32) * deviation
    if len(pieces) > 0:
        entries = levels(own_key, extent, pieces, -0.22, 0.18) * entries
    return jnp.clip(entries, min=-reach, max=reach).astype(kind)


def heavy_noise(key, dims, width, limit, pieces, heavy, kind=jnp.bfloat16):
    values = width * jax.random.normal(key, dims, jnp.float32)
    if pieces:
        values = values * levels(key, dims, pieces, -0.22, 0.18)
    return jnp.clip(strengthened(values, jax.random.fold_in(key, 3), *heavy), -limit, limit).astype(kind)


def setup_inputs(seed: int = 0) -> dict:
    seeds = jax.random.split(jax.random.key(seed), 8)
    return {
        "inputs": centred(seeds[0], (NEW, D), 1.0, 6.0, ((0, 8), (1, 4))),
        "gain": jnp.clip(1.0 + 0.15 * jax.random.normal(seeds[1], (D,), jnp.float32), 0.25, 1.75),
        "w_in": centred(seeds[2], (D, 3, D), D ** -0.5, 0.09375, ((2, 4),)),
        "w_out": heavy_noise(seeds[3], (D, D), D ** -0.5, 0.125, ((0, 4),), (0, 1, 4, 2.0)),
        "history": centred(seeds[4], (H, 2, D), 1.0, 6.0, ((0, 8), (2, 4))),
        "filt_far": centred(seeds[5], (H, 2, D), (H + NEW) ** -0.5, 0.125, ((0, 8), (2, 4))),
        "filt_near": centred(seeds[6], (NEW, 2, D), (H + NEW) ** -0.5, 0.125, ((2, 4),)),
    }


def split_blocks(array, groups, chan_block):
    return array.reshape(array.shape[0], groups, chan_block).transpose(1, 0, 2)

def history_conv(taps_far, taps_near, past_rows, fresh_rows):
    taps = jnp.concatenate([taps_far, taps_near], 0).astype(jnp.float32)[::-1]
    signal = jnp.concatenate([past_rows, fresh_rows], 0).astype(jnp.float32)
    total_len = taps.shape[0]
    fresh_len = fresh_rows.shape[0]
    chan_block = min(taps.shape[1], 256)
    groups = taps.shape[1] // chan_block

    def one_block(pair):
        kernel_block, signal_block = pair
        spectra = jnp.fft.rfft(kernel_block, n=2 * total_len, axis=0) * jnp.fft.rfft(signal_block, n=2 * total_len, axis=0)
        circular = jnp.fft.irfft(spectra, n=2 * total_len, axis=0)
        return circular[total_len - fresh_len:total_len]
    blocks = lax.map(one_block, (split_blocks(taps, groups, chan_block), split_blocks(signal, groups, chan_block)))
    return blocks.transpose(1, 0, 2).reshape(fresh_len, groups * chan_block)

def reference(inputs, gain, w_in, w_out, history, filt_far, filt_near):
    features = inputs.astype(jnp.float32)
    mean_sq = lax.optimization_barrier(jnp.mean(features * features, axis=-1, keepdims=True))
    normed = (features * lax.rsqrt(mean_sq + 1e-06) * gain).astype(jnp.bfloat16)
    model_width = w_in.shape[0]
    projected = jnp.dot(normed, w_in.reshape(model_width, 3 * model_width), preferred_element_type=jnp.float32)
    projected = projected.reshape(normed.shape[0], 3, model_width)
    values = projected[:, 0].astype(jnp.bfloat16)
    gate_one = projected[:, 1].astype(jnp.bfloat16)
    gate_two = projected[:, 2].astype(jnp.bfloat16)
    first_conv = history_conv(filt_far[:, 0], filt_near[:, 0], history[:, 0], values)
    gated = (gate_one.astype(jnp.float32) * first_conv).astype(jnp.bfloat16)
    second_conv = history_conv(filt_far[:, 1], filt_near[:, 1], history[:, 1], gated)
    mixed_in = (gate_two.astype(jnp.float32) * second_conv).astype(jnp.bfloat16)
    mixed = jnp.dot(mixed_in, w_out, preferred_element_type=jnp.float32).astype(jnp.bfloat16)
    return (mixed, gated)
```

```python
import jax
import jax.numpy as jnp
import numpy as np
from jax import lax
from jax.sharding import PartitionSpec as P


def split_pair(matrix):
    high = matrix.astype(jnp.bfloat16)
    low = (matrix - high.astype(np.float64)).astype(jnp.bfloat16)
    return high, low


def transforms(block):
    angle = np.pi * (np.arange(block)[:, None] + 0.5) * np.arange(block)[None, :] / block
    forward = np.concatenate([np.cos(angle), -np.sin(angle)], 0)
    inverse = np.concatenate([np.cos(angle), -np.sin(angle)], 0).T[::-1] / block
    sign = np.where(np.arange(block) % 2 == 0, 1.0, -1.0).astype(np.float32)
    return split_pair(forward), split_pair(inverse), sign


def times(a, b):
    return jnp.dot(a, b, preferred_element_type=jnp.float32)


def per_device(inputs, gain, w_in, w_out, history, filt_far, filt_near):
    chan_width = inputs.shape[1]
    block = filt_near.shape[0]
    ctx_index = lax.axis_index("ctx")
    ctx_count = lax.axis_size("ctx")
    column_count = chan_width // ctx_count
    (fwd_hi, fwd_lo), (inv_hi, inv_lo), sign = transforms(block)
    sign = jnp.asarray(sign)[None, :, None]

    gathered = lax.all_gather(inputs, "chan", axis=1, tiled=True)
    features = gathered.astype(jnp.float32)
    mean_sq = jnp.mean(features * features, axis=-1, keepdims=True)
    normed = (features * lax.rsqrt(mean_sq + 1e-06) * gain).astype(jnp.bfloat16)
    weights = w_in.transpose(1, 0, 2)
    fresh = [
        lax.all_to_all(
            times(normed, weights[i]).astype(jnp.bfloat16),
            "ctx",
            split_axis=1,
            concat_axis=0,
            tiled=True,
        )
        for i in range(3)
    ]
    value_cols, first_gate, second_gate = fresh
    hist_cols, far_cols = (
        lax.all_to_all(history, "ctx", split_axis=2, concat_axis=0, tiled=True),
        lax.all_to_all(filt_far, "ctx", split_axis=2, concat_axis=0, tiled=True),
    )
    near_cols = lax.dynamic_slice_in_dim(filt_near, ctx_index * column_count, column_count, 2)
    old_blocks = hist_cols.shape[0] // block

    def forward(rows):
        return times(fwd_hi, rows) + times(fwd_lo, rows)

    def as_columns(rows):
        count = rows.shape[0] // block
        return (
            rows.reshape(count, block, 2, column_count)
            .transpose(1, 2, 0, 3)
            .reshape(block, 2 * count * column_count)
        )

    def as_spectra(freq, count):
        return freq.reshape(2, block, 2, count, column_count).transpose(3, 0, 1, 2, 4)

    hist_f = as_spectra(forward(as_columns(hist_cols)), old_blocks)
    far_f = as_spectra(forward(as_columns(far_cols)), old_blocks)
    near_f = as_spectra(forward(as_columns(near_cols)), 1)
    filt_f = jnp.concatenate([far_f, near_f], 0)
    tap_re, tap_im = filt_f[:, 0], filt_f[:, 1]
    turn = jnp.asarray(sign)[..., None]
    win_re = tap_re[:-1] + turn * tap_im[1:]
    win_im = tap_im[:-1] - turn * tap_re[1:]
    old_re, old_im = hist_f[:, 0], hist_f[:, 1]
    sum_re = jnp.sum(win_re * old_re + win_im * old_im, 0)
    sum_im = jnp.sum(win_im * old_re - win_re * old_im, 0)

    def whole_conv(which, rows):
        new_f = forward(rows)
        new_re, new_im = new_f[:block], new_f[block:]
        near_re, near_im = near_f[0, 0, :, which], near_f[0, 1, :, which]
        total = jnp.concatenate(
            [
                sum_re[:, which] + near_re * new_re + near_im * new_im,
                sum_im[:, which] + near_im * new_re - near_re * new_im,
            ],
            0,
        )
        high = lax.reduce_precision(total, 8, 7)
        low = (total - high).astype(jnp.bfloat16)
        high = high.astype(jnp.bfloat16)
        return times(inv_hi, high) + times(inv_lo, high) + times(inv_hi, low)

    first_full = whole_conv(0, value_cols)
    gated_cols = (first_gate.astype(jnp.float32) * first_full).astype(jnp.bfloat16)
    second_full = whole_conv(1, gated_cols)
    mixed_cols = (second_gate.astype(jnp.float32) * second_full).astype(jnp.bfloat16)
    gated, mixed_in = (
        lax.all_to_all(gated_cols, "ctx", split_axis=0, concat_axis=1, tiled=True),
        lax.all_to_all(mixed_cols, "ctx", split_axis=0, concat_axis=1, tiled=True),
    )
    partial_out = jnp.dot(mixed_in, w_out, preferred_element_type=jnp.float32)
    mixed = lax.psum_scatter(partial_out, "chan", scatter_dimension=1, tiled=True).astype(
        jnp.bfloat16
    )
    return (mixed, gated)


def solution(mesh):
    placed = (
        P("ctx", "chan"),
        P(),
        P(None, None, "chan"),
        P("chan", None),
        P("ctx", None, "chan"),
        P("ctx", None, "chan"),
        P(None, None, "chan"),
    )
    return jax.shard_map(
        per_device,
        mesh=mesh,
        in_specs=placed,
        out_specs=(P("ctx", "chan"), P("ctx", "chan")),
        check_vma=False,
    )
```

```python
import functools

import jax
import jax.numpy as jnp
import numpy as np
from jax import lax
from jax.experimental import pallas as pl
from jax.experimental.pallas import tpu as pltpu
from jax.sharding import PartitionSpec as P


def split_pair(matrix):
    high = matrix.astype(jnp.bfloat16)
    low = (matrix - high.astype(np.float64)).astype(jnp.bfloat16)
    return high, low


def transforms(block):
    angle = np.pi * (np.arange(block)[:, None] + 0.5) * np.arange(block)[None, :] / block
    forward = np.concatenate([np.cos(angle), -np.sin(angle)], 0)
    inverse = np.concatenate([np.cos(angle), -np.sin(angle)], 0).T[::-1] / block
    sign = np.where(np.arange(block) % 2 == 0, 1.0, -1.0).astype(np.float32)
    return split_pair(forward), split_pair(inverse), sign


def times(a, b):
    return jnp.dot(a, b, preferred_element_type=jnp.float32)


def plain_layer(inputs, gain, w_in, w_out, history, filt_far, filt_near):
    chan_width = inputs.shape[1]
    block = filt_near.shape[0]
    ctx_index = lax.axis_index("ctx")
    ctx_count = lax.axis_size("ctx")
    column_count = chan_width // ctx_count
    (fwd_hi, fwd_lo), (inv_hi, inv_lo), sign = transforms(block)
    sign = jnp.asarray(sign)[None, :, None]

    gathered = lax.all_gather(inputs, "chan", axis=1, tiled=True)
    features = gathered.astype(jnp.float32)
    mean_sq = jnp.mean(features * features, axis=-1, keepdims=True)
    normed = (features * lax.rsqrt(mean_sq + 1e-06) * gain).astype(jnp.bfloat16)
    weights = w_in.transpose(1, 0, 2)
    fresh = [
        lax.all_to_all(
            times(normed, weights[i]).astype(jnp.bfloat16),
            "ctx",
            split_axis=1,
            concat_axis=0,
            tiled=True,
        )
        for i in range(3)
    ]
    value_cols, first_gate, second_gate = fresh
    hist_cols, far_cols = (
        lax.all_to_all(history, "ctx", split_axis=2, concat_axis=0, tiled=True),
        lax.all_to_all(filt_far, "ctx", split_axis=2, concat_axis=0, tiled=True),
    )
    near_cols = lax.dynamic_slice_in_dim(filt_near, ctx_index * column_count, column_count, 2)
    old_blocks = hist_cols.shape[0] // block

    def forward(rows):
        return times(fwd_hi, rows) + times(fwd_lo, rows)

    def as_columns(rows):
        count = rows.shape[0] // block
        return (
            rows.reshape(count, block, 2, column_count)
            .transpose(1, 2, 0, 3)
            .reshape(block, 2 * count * column_count)
        )

    def as_spectra(freq, count):
        return freq.reshape(2, block, 2, count, column_count).transpose(3, 0, 1, 2, 4)

    hist_f = as_spectra(forward(as_columns(hist_cols)), old_blocks)
    far_f = as_spectra(forward(as_columns(far_cols)), old_blocks)
    near_f = as_spectra(forward(as_columns(near_cols)), 1)
    filt_f = jnp.concatenate([far_f, near_f], 0)
    tap_re, tap_im = filt_f[:, 0], filt_f[:, 1]
    turn = jnp.asarray(sign)[..., None]
    win_re = tap_re[:-1] + turn * tap_im[1:]
    win_im = tap_im[:-1] - turn * tap_re[1:]
    old_re, old_im = hist_f[:, 0], hist_f[:, 1]
    sum_re = jnp.sum(win_re * old_re + win_im * old_im, 0)
    sum_im = jnp.sum(win_im * old_re - win_re * old_im, 0)

    def whole_conv(which, rows):
        new_f = forward(rows)
        new_re, new_im = new_f[:block], new_f[block:]
        near_re, near_im = near_f[0, 0, :, which], near_f[0, 1, :, which]
        total = jnp.concatenate(
            [
                sum_re[:, which] + near_re * new_re + near_im * new_im,
                sum_im[:, which] + near_im * new_re - near_re * new_im,
            ],
            0,
        )
        high = lax.reduce_precision(total, 8, 7)
        low = (total - high).astype(jnp.bfloat16)
        high = high.astype(jnp.bfloat16)
        return times(inv_hi, high) + times(inv_lo, high) + times(inv_hi, low)

    first_full = whole_conv(0, value_cols)
    gated_cols = (first_gate.astype(jnp.float32) * first_full).astype(jnp.bfloat16)
    second_full = whole_conv(1, gated_cols)
    mixed_cols = (second_gate.astype(jnp.float32) * second_full).astype(jnp.bfloat16)
    gated, mixed_in = (
        lax.all_to_all(gated_cols, "ctx", split_axis=0, concat_axis=1, tiled=True),
        lax.all_to_all(mixed_cols, "ctx", split_axis=0, concat_axis=1, tiled=True),
    )
    partial_out = jnp.dot(mixed_in, w_out, preferred_element_type=jnp.float32)
    mixed = lax.psum_scatter(partial_out, "chan", scatter_dimension=1, tiled=True).astype(
        jnp.bfloat16
    )
    return (mixed, gated)


MESH = pl.DeviceIdType.MESH


def layer_kernel(
    n, cn, inputs, gain, w_in, w_out, history, filt_far, filt_near, fwd_hi, fwd_lo, inv_hi, inv_lo,
    mixed, gated,
    x_all, normed, win, wout, h_stage, f_stage, h_all, f_all, near, wide, h_spec, f_spec, total,
    acc, fresh_out, fresh_all, back_out, g_all, m_all, m_full, part, part_all,
    x_local, x_send, x_recv, hs_sem, fs_sem, win_sem, wout_sem, near_sem,
    h_send, h_recv, f_send, f_recv, v_send, v_recv, g_send, g_recv, m_send, m_recv, p_send, p_recv,
):
    me = lax.axis_index("ctx")
    mine = lax.axis_index("chan")
    rows, width = inputs.shape
    block = history.shape[0]
    cols = width // n

    def lanes(d):
        return pl.ds(pl.multiple_of(d * cols, 128), cols)

    def remote(src, dst, send, recv, where):
        return pltpu.make_async_remote_copy(
            src_ref=src, dst_ref=dst, send_sem=send, recv_sem=recv,
            device_id=where, device_id_type=MESH,
        )

    def ctx_peer(s):
        return lax.rem(me + s, n)

    def chan_peer(s):
        return lax.rem(mine + s, cn)

    x_copy = pltpu.make_async_copy(inputs, x_all.at[mine], x_local)
    x_copy.start()
    h_local, f_local = [], []
    for s in range(n):
        d = ctx_peer(s)
        h_to = h_all.at[me] if s == 0 else h_stage.at[s - 1]
        f_to = f_all.at[me] if s == 0 else f_stage.at[s - 1]
        h_local.append(pltpu.make_async_copy(history.at[:, :, lanes(d)], h_to, hs_sem.at[s]))
        f_local.append(pltpu.make_async_copy(filt_far.at[:, :, lanes(d)], f_to, fs_sem.at[s]))
    near_copy = pltpu.make_async_copy(filt_near.at[:, :, lanes(me)], near, near_sem)
    order = list(range(2, n)) + [1, 0]
    for s in order:
        h_local[s].start()
        f_local[s].start()
    near_copy.start()
    win_copies = []
    for i in range(3):
        for j in range(cn):
            copy = pltpu.make_async_copy(
                w_in.at[i, pl.ds(j * width, width)], win.at[i * cn + j], win_sem.at[i * cn + j]
            )
            copy.start()
            win_copies.append(copy)
    wout_copies = []
    for j in range(cn):
        copy = pltpu.make_async_copy(
            w_out.at[:, pl.ds(j * width, width)], wout.at[j], wout_sem.at[j]
        )
        copy.start()
        wout_copies.append(copy)

    barrier = pltpu.get_barrier_semaphore()
    for s in range(1, n):
        pl.semaphore_signal(barrier, inc=1, device_id={"ctx": ctx_peer(s)}, device_id_type=MESH)
    for s in range(1, cn):
        pl.semaphore_signal(barrier, inc=1, device_id={"chan": chan_peer(s)}, device_id_type=MESH)
    pl.semaphore_wait(barrier, n + cn - 2)

    x_copies = []
    for s in range(1, cn):
        copy = remote(
            inputs, x_all.at[mine], x_send.at[s], x_recv.at[s], {"chan": chan_peer(s)}
        )
        copy.start()
        x_copies.append(copy)
    h_copies, f_copies = [None] * n, [None] * n
    for s in order[:-1]:
        where = {"ctx": ctx_peer(s)}
        h_local[s].wait()
        h_copies[s] = remote(h_stage.at[s - 1], h_all.at[me], h_send.at[s], h_recv.at[s], where)
        h_copies[s].start()
        f_local[s].wait()
        f_copies[s] = remote(f_stage.at[s - 1], f_all.at[me], f_send.at[s], f_recv.at[s], where)
        f_copies[s].start()

    def forward(x):
        return times(fwd_hi[...], x) + times(fwd_lo[...], x)

    def halves(ref):
        wide[...] = ref.reshape(2 * block, cols)[...].astype(jnp.float32)
        return [
            wide[pl.ds(c, block, stride=2), :].astype(jnp.bfloat16) for c in range(2)
        ]

    def transform(k):
        x = jnp.concatenate(halves(h_all.at[k]) + halves(f_all.at[k]), axis=1)
        spec = forward(x)
        h_spec[k] = spec[:, : 2 * cols]
        f_spec[k] = spec[:, 2 * cols :]

    h_local[0].wait()
    f_local[0].wait()
    near_copy.wait()
    f_spec[n] = forward(jnp.concatenate(halves(near), axis=1))
    transform(me)

    x_copy.wait()
    for copy in x_copies:
        copy.wait_recv()
    square = jnp.zeros((rows, 1), jnp.float32)
    for j in range(cn):
        part_x = x_all[j].astype(jnp.float32)
        square = square + jnp.sum(part_x * part_x, axis=-1, keepdims=True)
    scale = lax.rsqrt(square / (cn * width) + 1e-06)
    for j in range(cn):
        normed[j] = (x_all[j].astype(jnp.float32) * scale * gain[j : j + 1, :]).astype(jnp.bfloat16)

    for i in range(3):
        for j in range(cn):
            win_copies[i * cn + j].wait()

        @pl.loop(0, n // 2 if n % 2 == 0 else n)
        def _(q):
            step = 2 if n % 2 == 0 else 1
            span = step * cols
            at = pl.ds(pl.multiple_of(q * span, 128), span)
            proj = times(normed[0], win[i * cn, :, at])
            for j in range(1, cn):
                proj = proj + times(normed[j], win[i * cn + j, :, at])
            for p in range(step):
                fresh_out[q * step + p, i] = proj[:, p * cols : (p + 1) * cols].astype(jnp.bfloat16)

    v_local = pltpu.make_async_copy(fresh_out.at[me], fresh_all.at[me], v_recv.at[0])
    v_local.start()
    v_copies = []
    for s in range(1, n):
        d = ctx_peer(s)
        copy = remote(
            fresh_out.at[d], fresh_all.at[me], v_send.at[s], v_recv.at[s], {"ctx": d}
        )
        copy.start()
        v_copies.append(copy)

    for s in [1] + list(range(2, n)):
        h_copies[s].wait_recv()
        f_copies[s].wait_recv()
        transform(lax.rem(me + n - s, n))

    chunk = 32

    @pl.loop(0, block // chunk)
    def _(r):
        low = pl.ds(pl.multiple_of(r * chunk, chunk), chunk)
        high = pl.ds(pl.multiple_of(block + r * chunk, chunk), chunk)
        odd = lax.broadcasted_iota(jnp.int32, (chunk, 2 * cols), 0) % 2
        turn = 1.0 - 2.0 * odd.astype(jnp.float32)
        sum_re = jnp.zeros((chunk, 2 * cols), jnp.float32)
        sum_im = jnp.zeros((chunk, 2 * cols), jnp.float32)
        for k in range(n):
            win_re = f_spec[k, low, :] + turn * f_spec[k + 1, high, :]
            win_im = f_spec[k, high, :] - turn * f_spec[k + 1, low, :]
            old_re, old_im = h_spec[k, low, :], h_spec[k, high, :]
            sum_re = sum_re + win_re * old_re + win_im * old_im
            sum_im = sum_im + win_im * old_re - win_re * old_im
        acc[low, :] = sum_re
        acc[high, :] = sum_im

    def whole_conv(which, values):
        at = slice(which * cols, (which + 1) * cols)
        new = forward(values)
        new_re, new_im = new[:block], new[block:]
        near_re, near_im = f_spec[n, :block, at], f_spec[n, block:, at]
        all_re = acc[:block, at] + near_re * new_re + near_im * new_im
        all_im = acc[block:, at] + near_im * new_re - near_re * new_im
        whole = jnp.concatenate([all_re, all_im], axis=0)
        high = whole.astype(jnp.bfloat16)
        low = (whole - high.astype(jnp.float32)).astype(jnp.bfloat16)
        both = times(inv_hi[...], jnp.concatenate([high, low], axis=1))
        return both[:, :cols] + both[:, cols:] + times(inv_lo[...], high)

    def send_back(index, every, send, recv):
        local = pltpu.make_async_copy(back_out.at[index, me], every.at[me], recv.at[0])
        local.start()
        copies = []
        for s in range(1, n):
            d = ctx_peer(s)
            copy = remote(
                back_out.at[index, d], every.at[me], send.at[s], recv.at[s], {"ctx": d}
            )
            copy.start()
            copies.append(copy)
        return local, copies

    v_local.wait()
    for copy in v_copies:
        copy.wait_recv()
    fresh_rows = n * rows
    first = whole_conv(0, fresh_all[:, 0].reshape(fresh_rows, cols))
    gate_one = fresh_all[:, 1].reshape(fresh_rows, cols).astype(jnp.float32)
    gated_cols = (gate_one * first).astype(jnp.bfloat16)
    back_out[0] = gated_cols.reshape(n, rows, cols)
    g_local, g_copies = send_back(0, g_all, g_send, g_recv)
    second = whole_conv(1, gated_cols)
    gate_two = fresh_all[:, 2].reshape(fresh_rows, cols).astype(jnp.float32)
    back_out[1] = (gate_two * second).astype(jnp.bfloat16).reshape(n, rows, cols)
    m_local, m_copies = send_back(1, m_all, m_send, m_recv)

    g_local.wait()
    for copy in g_copies:
        copy.wait_recv()
    for j in range(n):
        gated[:, j * cols : (j + 1) * cols] = g_all[j]
    for copy in wout_copies:
        copy.wait()
    m_local.wait()
    for copy in m_copies:
        copy.wait_recv()
    for j in range(n):
        m_full[:, j * cols : (j + 1) * cols] = m_all[j]
    p_copies = []
    for s in list(range(1, cn)) + [0]:
        d = chan_peer(s)
        part[s] = times(m_full[...], wout[d])
        if s > 0:
            copy = remote(part.at[s], part_all.at[s], p_send.at[s], p_recv.at[s], {"chan": d})
            copy.start()
            p_copies.append(copy)
    result = part[0]
    for s, copy in enumerate(p_copies):
        copy.wait_recv()
        result = result + part_all[s + 1]
    mixed[...] = result.astype(jnp.bfloat16)

    for copy in x_copies + h_copies[1:] + f_copies[1:] + v_copies + g_copies + m_copies + p_copies:
        copy.wait_send()


def fused_layer(inputs, gain, w_in, w_out, history, filt_far, filt_near):
    n, cn = lax.axis_size("ctx"), lax.axis_size("chan")
    rows, width = inputs.shape
    block = history.shape[0]
    cols = width // n
    (fwd_hi, fwd_lo), (inv_hi, inv_lo), _ = transforms(block)
    f32, bf16 = jnp.float32, jnp.bfloat16
    vmem = pl.BlockSpec(memory_space=pltpu.VMEM)
    anywhere = pl.BlockSpec(memory_space=pl.ANY)
    dma = pltpu.SemaphoreType.DMA
    return pl.pallas_call(
        functools.partial(layer_kernel, n, cn),
        out_shape=(jax.ShapeDtypeStruct((rows, width), bf16),) * 2,
        in_specs=[anywhere, vmem] + [anywhere] * 5 + [vmem] * 4,
        out_specs=(vmem, vmem),
        scratch_shapes=[
            pltpu.VMEM((cn, rows, width), bf16),
            pltpu.VMEM((cn, rows, width), bf16),
            pltpu.VMEM((3 * cn, width, width), bf16),
            pltpu.VMEM((cn, width, width), bf16),
            pltpu.VMEM((n - 1, block, 2, cols), bf16),
            pltpu.VMEM((n - 1, block, 2, cols), bf16),
            pltpu.VMEM((n, block, 2, cols), bf16),
            pltpu.VMEM((n, block, 2, cols), bf16),
            pltpu.VMEM((block, 2, cols), bf16),
            pltpu.VMEM((2 * block, cols), f32),
            pltpu.VMEM((n, 2 * block, 2 * cols), f32),
            pltpu.VMEM((n + 1, 2 * block, 2 * cols), f32),
            pltpu.VMEM((8, 128), f32),
            pltpu.VMEM((2 * block, 2 * cols), f32),
            pltpu.VMEM((n, 3, rows, cols), bf16),
            pltpu.VMEM((n, 3, rows, cols), bf16),
            pltpu.VMEM((2, n, rows, cols), bf16),
            pltpu.VMEM((n, rows, cols), bf16),
            pltpu.VMEM((n, rows, cols), bf16),
            pltpu.VMEM((rows, width), bf16),
            pltpu.VMEM((cn, rows, width), f32),
            pltpu.VMEM((cn, rows, width), f32),
            dma, dma((cn,)), dma((cn,)), dma((n,)), dma((n,)), dma((3 * cn,)), dma((cn,)), dma,
        ]
        + [dma((n,))] * 10
        + [dma((cn,))] * 2,
        compiler_params=pltpu.CompilerParams(
            collective_id=0, has_side_effects=True, vmem_limit_bytes=60 * 1024 * 1024
        ),
    )(
        inputs, gain.reshape(cn, width), w_in.transpose(1, 0, 2), w_out, history, filt_far,
        filt_near, fwd_hi, fwd_lo, inv_hi, inv_lo,
    )


def per_device(inputs, gain, w_in, w_out, history, filt_far, filt_near):
    n = lax.axis_size("ctx")
    rows, width = inputs.shape
    fits = (
        width % (128 * n) == 0
        and rows % 16 == 0
        and history.shape[0] == filt_near.shape[0] == n * rows
    )
    layer = fused_layer if fits else plain_layer
    return layer(inputs, gain, w_in, w_out, history, filt_far, filt_near)


def solution(mesh):
    placed = (
        P("ctx", "chan"),
        P(),
        P(None, None, "chan"),
        P("chan", None),
        P("ctx", None, "chan"),
        P("ctx", None, "chan"),
        P(None, None, "chan"),
    )
    return jax.shard_map(
        per_device,
        mesh=mesh,
        in_specs=placed,
        out_specs=(P("ctx", "chan"), P("ctx", "chan")),
        check_vma=False,
    )
```

```python
import functools

import jax
import jax.numpy as jnp
import numpy as np
from jax import lax
from jax.experimental import pallas as pl
from jax.experimental.pallas import tpu as pltpu
from jax.sharding import PartitionSpec as P


def split_pair(matrix):
    high = matrix.astype(jnp.bfloat16)
    low = (matrix - high.astype(np.float64)).astype(jnp.bfloat16)
    return high, low


def transforms(block):
    angle = np.pi * (np.arange(block)[:, None] + 0.5) * np.arange(block)[None, :] / block
    forward = np.concatenate([np.cos(angle), -np.sin(angle)], 0)
    inverse = np.concatenate([np.cos(angle), -np.sin(angle)], 0).T[::-1] / block
    sign = np.where(np.arange(block) % 2 == 0, 1.0, -1.0).astype(np.float32)
    return split_pair(forward), split_pair(inverse), sign


def times(a, b):
    return jnp.dot(a, b, preferred_element_type=jnp.float32)


def plain_layer(inputs, gain, w_in, w_out, history, filt_far, filt_near):
    chan_width = inputs.shape[1]
    block = filt_near.shape[0]
    ctx_index = lax.axis_index("ctx")
    ctx_count = lax.axis_size("ctx")
    column_count = chan_width // ctx_count
    (fwd_hi, fwd_lo), (inv_hi, inv_lo), sign = transforms(block)
    sign = jnp.asarray(sign)[None, :, None]

    gathered = lax.all_gather(inputs, "chan", axis=1, tiled=True)
    features = gathered.astype(jnp.float32)
    mean_sq = jnp.mean(features * features, axis=-1, keepdims=True)
    normed = (features * lax.rsqrt(mean_sq + 1e-06) * gain).astype(jnp.bfloat16)
    weights = w_in.transpose(1, 0, 2)
    fresh = [
        lax.all_to_all(
            times(normed, weights[i]).astype(jnp.bfloat16),
            "ctx",
            split_axis=1,
            concat_axis=0,
            tiled=True,
        )
        for i in range(3)
    ]
    value_cols, first_gate, second_gate = fresh
    hist_cols, far_cols = (
        lax.all_to_all(history, "ctx", split_axis=2, concat_axis=0, tiled=True),
        lax.all_to_all(filt_far, "ctx", split_axis=2, concat_axis=0, tiled=True),
    )
    near_cols = lax.dynamic_slice_in_dim(filt_near, ctx_index * column_count, column_count, 2)
    old_blocks = hist_cols.shape[0] // block

    def forward(rows):
        return times(fwd_hi, rows) + times(fwd_lo, rows)

    def as_columns(rows):
        count = rows.shape[0] // block
        return (
            rows.reshape(count, block, 2, column_count)
            .transpose(1, 2, 0, 3)
            .reshape(block, 2 * count * column_count)
        )

    def as_spectra(freq, count):
        return freq.reshape(2, block, 2, count, column_count).transpose(3, 0, 1, 2, 4)

    hist_f = as_spectra(forward(as_columns(hist_cols)), old_blocks)
    far_f = as_spectra(forward(as_columns(far_cols)), old_blocks)
    near_f = as_spectra(forward(as_columns(near_cols)), 1)
    filt_f = jnp.concatenate([far_f, near_f], 0)
    tap_re, tap_im = filt_f[:, 0], filt_f[:, 1]
    turn = jnp.asarray(sign)[..., None]
    win_re = tap_re[:-1] + turn * tap_im[1:]
    win_im = tap_im[:-1] - turn * tap_re[1:]
    old_re, old_im = hist_f[:, 0], hist_f[:, 1]
    sum_re = jnp.sum(win_re * old_re + win_im * old_im, 0)
    sum_im = jnp.sum(win_im * old_re - win_re * old_im, 0)

    def whole_conv(which, rows):
        new_f = forward(rows)
        new_re, new_im = new_f[:block], new_f[block:]
        near_re, near_im = near_f[0, 0, :, which], near_f[0, 1, :, which]
        total = jnp.concatenate(
            [
                sum_re[:, which] + near_re * new_re + near_im * new_im,
                sum_im[:, which] + near_im * new_re - near_re * new_im,
            ],
            0,
        )
        high = lax.reduce_precision(total, 8, 7)
        low = (total - high).astype(jnp.bfloat16)
        high = high.astype(jnp.bfloat16)
        return times(inv_hi, high) + times(inv_lo, high) + times(inv_hi, low)

    first_full = whole_conv(0, value_cols)
    gated_cols = (first_gate.astype(jnp.float32) * first_full).astype(jnp.bfloat16)
    second_full = whole_conv(1, gated_cols)
    mixed_cols = (second_gate.astype(jnp.float32) * second_full).astype(jnp.bfloat16)
    gated, mixed_in = (
        lax.all_to_all(gated_cols, "ctx", split_axis=0, concat_axis=1, tiled=True),
        lax.all_to_all(mixed_cols, "ctx", split_axis=0, concat_axis=1, tiled=True),
    )
    partial_out = jnp.dot(mixed_in, w_out, preferred_element_type=jnp.float32)
    mixed = lax.psum_scatter(partial_out, "chan", scatter_dimension=1, tiled=True).astype(
        jnp.bfloat16
    )
    return (mixed, gated)


MESH = pl.DeviceIdType.MESH


def layer_kernel(
    n, cn, inputs, gain, w_in, w_out, history, filt_far, filt_near, fwd_hi, fwd_lo, inv_hi, inv_lo,
    out,
    x_all, normed, win, wout, h_stage, f_stage, h_all, f_all, near, wide, h_spec, f_spec,
    acc, fresh_out, fresh_all, back_out, g_all, m_all, m_full, part, part_all,
    x_local, x_send, x_recv, hs_sem, fs_sem, win_sem, wout_sem, near_sem,
    h_send, h_recv, f_send, f_recv, v_send, v_recv, g_send, g_recv, m_send, m_recv, p_send, p_recv,
):
    me = lax.axis_index("ctx")
    mine = lax.axis_index("chan")
    rows, width = inputs.shape
    block = history.shape[0]
    cols = width // n

    def lanes(d):
        return pl.ds(pl.multiple_of(d * cols, 128), cols)

    def remote(src, dst, send, recv, where):
        return pltpu.make_async_remote_copy(
            src_ref=src, dst_ref=dst, send_sem=send, recv_sem=recv,
            device_id=where, device_id_type=MESH,
        )

    def ctx_peer(s):
        return lax.rem(me + s, n)

    def chan_peer(s):
        return lax.rem(mine + s, cn)

    x_copy = pltpu.make_async_copy(inputs, x_all.at[mine], x_local)
    x_copy.start()
    h_local, f_local = [], []
    for s in range(n):
        d = ctx_peer(s)
        h_to = h_all.at[me] if s == 0 else h_stage.at[s - 1]
        f_to = f_all.at[me] if s == 0 else f_stage.at[s - 1]
        h_local.append(pltpu.make_async_copy(history.at[:, :, lanes(d)], h_to, hs_sem.at[s]))
        f_local.append(pltpu.make_async_copy(filt_far.at[:, :, lanes(d)], f_to, fs_sem.at[s]))
    near_copy = pltpu.make_async_copy(filt_near.at[:, :, lanes(me)], near, near_sem)
    order = list(range(1, n)) + [0]
    for s in order:
        h_local[s].start()
        f_local[s].start()
    near_copy.start()
    win_copies = []
    for i in range(3):
        for j in range(cn):
            copy = pltpu.make_async_copy(
                w_in.at[i, pl.ds(j * width, width)], win.at[i * cn + j], win_sem.at[i * cn + j]
            )
            copy.start()
            win_copies.append(copy)
    wout_copies = []
    for j in range(cn):
        copy = pltpu.make_async_copy(
            w_out.at[:, pl.ds(j * width, width)], wout.at[j], wout_sem.at[j]
        )
        copy.start()
        wout_copies.append(copy)

    barrier = pltpu.get_barrier_semaphore()
    for s in range(1, n):
        pl.semaphore_signal(barrier, inc=1, device_id={"ctx": ctx_peer(s)}, device_id_type=MESH)
    for s in range(1, cn):
        pl.semaphore_signal(barrier, inc=1, device_id={"chan": chan_peer(s)}, device_id_type=MESH)
    pl.semaphore_wait(barrier, n + cn - 2)

    x_copies = []
    for s in range(1, cn):
        copy = remote(
            inputs, x_all.at[mine], x_send.at[s], x_recv.at[s], {"chan": chan_peer(s)}
        )
        copy.start()
        x_copies.append(copy)
    h_copies, f_copies = [None] * n, [None] * n
    for s in order[:-1]:
        where = {"ctx": ctx_peer(s)}
        h_local[s].wait()
        h_copies[s] = remote(h_stage.at[s - 1], h_all.at[me], h_send.at[s], h_recv.at[s], where)
        h_copies[s].start()
        f_local[s].wait()
        f_copies[s] = remote(f_stage.at[s - 1], f_all.at[me], f_send.at[s], f_recv.at[s], where)
        f_copies[s].start()

    def forward(x):
        return times(fwd_hi[...], x) + times(fwd_lo[...], x)

    def halves(ref):
        wide[...] = ref.reshape(2 * block, cols)[...].astype(jnp.float32)
        return [
            wide[pl.ds(c, block, stride=2), :].astype(jnp.bfloat16) for c in range(2)
        ]

    def transform(k):
        x = jnp.concatenate(halves(h_all.at[k]) + halves(f_all.at[k]), axis=1)
        spec = forward(x)
        h_spec[k] = spec[:, : 2 * cols]
        f_spec[k] = spec[:, 2 * cols :]

    h_local[0].wait()
    f_local[0].wait()
    near_copy.wait()
    f_spec[n] = forward(jnp.concatenate(halves(near), axis=1))
    transform(me)

    x_copy.wait()
    for copy in x_copies:
        copy.wait_recv()
    square = jnp.zeros((rows, 1), jnp.float32)
    for j in range(cn):
        part_x = x_all[j].astype(jnp.float32)
        square = square + jnp.sum(part_x * part_x, axis=-1, keepdims=True)
    scale = lax.rsqrt(square / (cn * width) + 1e-06)
    for j in range(cn):
        normed[j] = (x_all[j].astype(jnp.float32) * scale * gain[:, j * width : (j + 1) * width]).astype(jnp.bfloat16)

    for i in range(3):
        for j in range(cn):
            win_copies[i * cn + j].wait()

        @pl.loop(0, n // 2 if n % 2 == 0 else n)
        def _(q):
            step = 2 if n % 2 == 0 else 1
            span = step * cols
            at = pl.ds(pl.multiple_of(q * span, 128), span)
            proj = times(normed[0], win[i * cn, :, at])
            for j in range(1, cn):
                proj = proj + times(normed[j], win[i * cn + j, :, at])
            for p in range(step):
                fresh_out[q * step + p, i] = proj[:, p * cols : (p + 1) * cols].astype(jnp.bfloat16)

    v_local = pltpu.make_async_copy(fresh_out.at[me], fresh_all.at[me], v_recv.at[0])
    v_local.start()
    v_copies = []
    for s in range(1, n):
        d = ctx_peer(s)
        copy = remote(
            fresh_out.at[d], fresh_all.at[me], v_send.at[s], v_recv.at[s], {"ctx": d}
        )
        copy.start()
        v_copies.append(copy)

    chunk = 32

    def add_term(k, first):
        @pl.loop(0, block // chunk)
        def _(r):
            low = pl.ds(pl.multiple_of(r * chunk, chunk), chunk)
            high = pl.ds(pl.multiple_of(block + r * chunk, chunk), chunk)
            odd = lax.broadcasted_iota(jnp.int32, (chunk, 2 * cols), 0) % 2
            turn = 1.0 - 2.0 * odd.astype(jnp.float32)
            win_re = f_spec[k, low, :] + turn * f_spec[k + 1, high, :]
            win_im = f_spec[k, high, :] - turn * f_spec[k + 1, low, :]
            old_re, old_im = h_spec[k, low, :], h_spec[k, high, :]
            sum_re = win_re * old_re + win_im * old_im
            sum_im = win_im * old_re - win_re * old_im
            if not first:
                sum_re = sum_re + acc[low, :]
                sum_im = sum_im + acc[high, :]
            acc[low, :] = sum_re
            acc[high, :] = sum_im

    def add_fresh(which, values):
        at = slice(which * cols, (which + 1) * cols)
        new = forward(values)
        new_re, new_im = new[:block], new[block:]
        near_re, near_im = f_spec[n, :block, at], f_spec[n, block:, at]
        acc[:block, at] += near_re * new_re + near_im * new_im
        acc[block:, at] += near_im * new_re - near_re * new_im

    fresh_rows = n * rows
    for s in range(1, n):
        if s == n - 1:
            v_local.wait()
            for copy in v_copies:
                copy.wait_recv()
            add_fresh(0, fresh_all[:, 0].reshape(fresh_rows, cols))
        h_copies[s].wait_recv()
        f_copies[s].wait_recv()
        k = lax.rem(me + n - s, n)
        transform(k)
        add_term(k, s == 1)
    add_term(me, False)

    def inverse(which):
        whole = acc[:, which * cols : (which + 1) * cols]
        high = whole.astype(jnp.bfloat16)
        low = (whole - high.astype(jnp.float32)).astype(jnp.bfloat16)
        both = times(inv_hi[...], jnp.concatenate([high, low], axis=1))
        return both[:, :cols] + both[:, cols:] + times(inv_lo[...], high)

    def send_back(index, every, send, recv):
        local = pltpu.make_async_copy(back_out.at[index, me], every.at[me], recv.at[0])
        local.start()
        copies = []
        for s in range(1, n):
            d = ctx_peer(s)
            copy = remote(
                back_out.at[index, d], every.at[me], send.at[s], recv.at[s], {"ctx": d}
            )
            copy.start()
            copies.append(copy)
        return local, copies

    first = inverse(0)
    gate_one = fresh_all[:, 1].reshape(fresh_rows, cols).astype(jnp.float32)
    gated_cols = (gate_one * first).astype(jnp.bfloat16)
    back_out[0] = gated_cols.reshape(n, rows, cols)
    g_local, g_copies = send_back(0, g_all, g_send, g_recv)
    add_fresh(1, gated_cols)
    second = inverse(1)
    gate_two = fresh_all[:, 2].reshape(fresh_rows, cols).astype(jnp.float32)
    back_out[1] = (gate_two * second).astype(jnp.bfloat16).reshape(n, rows, cols)
    m_local, m_copies = send_back(1, m_all, m_send, m_recv)

    g_local.wait()
    for copy in g_copies:
        copy.wait_recv()
    for j in range(n):
        out[1, :, j * cols : (j + 1) * cols] = g_all[j]
    for copy in wout_copies:
        copy.wait()
    m_local.wait()
    for copy in m_copies:
        copy.wait_recv()
    for j in range(n):
        m_full[:, j * cols : (j + 1) * cols] = m_all[j]
    p_copies = []
    for s in list(range(1, cn)) + [0]:
        d = chan_peer(s)
        product = times(m_full[...], wout[d])
        if s > 0:
            part[s] = product.astype(jnp.bfloat16)
            copy = remote(part.at[s], part_all.at[s], p_send.at[s], p_recv.at[s], {"chan": d})
            copy.start()
            p_copies.append(copy)
    result = product
    for s, copy in enumerate(p_copies):
        copy.wait_recv()
        result = result + part_all[s + 1].astype(jnp.float32)
    out[0] = result.astype(jnp.bfloat16)

    for copy in x_copies + h_copies[1:] + f_copies[1:] + v_copies + g_copies + m_copies + p_copies:
        copy.wait_send()


def fused_layer(inputs, gain, w_in, w_out, history, filt_far, filt_near):
    n, cn = lax.axis_size("ctx"), lax.axis_size("chan")
    rows, width = inputs.shape
    block = history.shape[0]
    cols = width // n
    (fwd_hi, fwd_lo), (inv_hi, inv_lo), _ = transforms(block)
    f32, bf16 = jnp.float32, jnp.bfloat16
    vmem = pl.BlockSpec(memory_space=pltpu.VMEM)
    anywhere = pl.BlockSpec(memory_space=pl.ANY)
    dma = pltpu.SemaphoreType.DMA
    both = pl.pallas_call(
        functools.partial(layer_kernel, n, cn),
        out_shape=jax.ShapeDtypeStruct((2, rows, width), bf16),
        in_specs=[anywhere, vmem] + [anywhere] * 5 + [vmem] * 4,
        out_specs=vmem,
        scratch_shapes=[
            pltpu.VMEM((cn, rows, width), bf16),
            pltpu.VMEM((cn, rows, width), bf16),
            pltpu.VMEM((3 * cn, width, width), bf16),
            pltpu.VMEM((cn, width, width), bf16),
            pltpu.VMEM((n - 1, block, 2, cols), bf16),
            pltpu.VMEM((n - 1, block, 2, cols), bf16),
            pltpu.VMEM((n, block, 2, cols), bf16),
            pltpu.VMEM((n, block, 2, cols), bf16),
            pltpu.VMEM((block, 2, cols), bf16),
            pltpu.VMEM((2 * block, cols), f32),
            pltpu.VMEM((n, 2 * block, 2 * cols), f32),
            pltpu.VMEM((n + 1, 2 * block, 2 * cols), f32),
            pltpu.VMEM((2 * block, 2 * cols), f32),
            pltpu.VMEM((n, 3, rows, cols), bf16),
            pltpu.VMEM((n, 3, rows, cols), bf16),
            pltpu.VMEM((2, n, rows, cols), bf16),
            pltpu.VMEM((n, rows, cols), bf16),
            pltpu.VMEM((n, rows, cols), bf16),
            pltpu.VMEM((rows, width), bf16),
            pltpu.VMEM((cn, rows, width), bf16),
            pltpu.VMEM((cn, rows, width), bf16),
            dma, dma((cn,)), dma((cn,)), dma((n,)), dma((n,)), dma((3 * cn,)), dma((cn,)), dma,
        ]
        + [dma((n,))] * 10
        + [dma((cn,))] * 2,
        compiler_params=pltpu.CompilerParams(
            collective_id=0, has_side_effects=True, vmem_limit_bytes=60 * 1024 * 1024
        ),
    )(
        inputs, gain.reshape(1, cn * width), w_in.transpose(1, 0, 2), w_out, history, filt_far,
        filt_near, fwd_hi, fwd_lo, inv_hi, inv_lo,
    )
    return both[0], both[1]


def per_device(inputs, gain, w_in, w_out, history, filt_far, filt_near):
    n = lax.axis_size("ctx")
    rows, width = inputs.shape
    fits = (
        width % (128 * n) == 0
        and rows % 16 == 0
        and history.shape[0] == filt_near.shape[0] == n * rows
    )
    layer = fused_layer if fits else plain_layer
    return layer(inputs, gain, w_in, w_out, history, filt_far, filt_near)


def solution(mesh):
    placed = (
        P("ctx", "chan"),
        P(),
        P(None, None, "chan"),
        P("chan", None),
        P("ctx", None, "chan"),
        P("ctx", None, "chan"),
        P(None, None, "chan"),
    )
    return jax.shard_map(
        per_device,
        mesh=mesh,
        in_specs=placed,
        out_specs=(P("ctx", "chan"), P("ctx", "chan")),
        check_vma=False,
    )
```

```python
import functools

import jax
import jax.numpy as jnp
import numpy as np
from jax import lax
from jax.experimental import pallas as pl
from jax.experimental.pallas import tpu as pltpu
from jax.sharding import PartitionSpec as P


def split_pair(matrix):
    high = matrix.astype(jnp.bfloat16)
    low = (matrix - high.astype(np.float64)).astype(jnp.bfloat16)
    return high, low


def transforms(block):
    angle = np.pi * (np.arange(block)[:, None] + 0.5) * np.arange(block)[None, :] / block
    forward = np.concatenate([np.cos(angle), -np.sin(angle)], 0)
    inverse = np.concatenate([np.cos(angle), -np.sin(angle)], 0).T[::-1] / block
    sign = np.where(np.arange(block) % 2 == 0, 1.0, -1.0).astype(np.float32)
    return split_pair(forward), split_pair(inverse), sign


def times(a, b):
    return jnp.dot(a, b, preferred_element_type=jnp.float32)


def plain_layer(inputs, gain, w_in, w_out, history, filt_far, filt_near):
    chan_width = inputs.shape[1]
    block = filt_near.shape[0]
    ctx_index = lax.axis_index("ctx")
    ctx_count = lax.axis_size("ctx")
    column_count = chan_width // ctx_count
    (fwd_hi, fwd_lo), (inv_hi, inv_lo), sign = transforms(block)
    sign = jnp.asarray(sign)[None, :, None]

    gathered = lax.all_gather(inputs, "chan", axis=1, tiled=True)
    features = gathered.astype(jnp.float32)
    mean_sq = jnp.mean(features * features, axis=-1, keepdims=True)
    normed = (features * lax.rsqrt(mean_sq + 1e-06) * gain).astype(jnp.bfloat16)
    weights = w_in.transpose(1, 0, 2)
    fresh = [
        lax.all_to_all(
            times(normed, weights[i]).astype(jnp.bfloat16),
            "ctx",
            split_axis=1,
            concat_axis=0,
            tiled=True,
        )
        for i in range(3)
    ]
    value_cols, first_gate, second_gate = fresh
    hist_cols, far_cols = (
        lax.all_to_all(history, "ctx", split_axis=2, concat_axis=0, tiled=True),
        lax.all_to_all(filt_far, "ctx", split_axis=2, concat_axis=0, tiled=True),
    )
    near_cols = lax.dynamic_slice_in_dim(filt_near, ctx_index * column_count, column_count, 2)
    old_blocks = hist_cols.shape[0] // block

    def forward(rows):
        return times(fwd_hi, rows) + times(fwd_lo, rows)

    def as_columns(rows):
        count = rows.shape[0] // block
        return (
            rows.reshape(count, block, 2, column_count)
            .transpose(1, 2, 0, 3)
            .reshape(block, 2 * count * column_count)
        )

    def as_spectra(freq, count):
        return freq.reshape(2, block, 2, count, column_count).transpose(3, 0, 1, 2, 4)

    hist_f = as_spectra(forward(as_columns(hist_cols)), old_blocks)
    far_f = as_spectra(forward(as_columns(far_cols)), old_blocks)
    near_f = as_spectra(forward(as_columns(near_cols)), 1)
    filt_f = jnp.concatenate([far_f, near_f], 0)
    tap_re, tap_im = filt_f[:, 0], filt_f[:, 1]
    turn = jnp.asarray(sign)[..., None]
    win_re = tap_re[:-1] + turn * tap_im[1:]
    win_im = tap_im[:-1] - turn * tap_re[1:]
    old_re, old_im = hist_f[:, 0], hist_f[:, 1]
    sum_re = jnp.sum(win_re * old_re + win_im * old_im, 0)
    sum_im = jnp.sum(win_im * old_re - win_re * old_im, 0)

    def whole_conv(which, rows):
        new_f = forward(rows)
        new_re, new_im = new_f[:block], new_f[block:]
        near_re, near_im = near_f[0, 0, :, which], near_f[0, 1, :, which]
        total = jnp.concatenate(
            [
                sum_re[:, which] + near_re * new_re + near_im * new_im,
                sum_im[:, which] + near_im * new_re - near_re * new_im,
            ],
            0,
        )
        high = lax.reduce_precision(total, 8, 7)
        low = (total - high).astype(jnp.bfloat16)
        high = high.astype(jnp.bfloat16)
        return times(inv_hi, high) + times(inv_lo, high) + times(inv_hi, low)

    first_full = whole_conv(0, value_cols)
    gated_cols = (first_gate.astype(jnp.float32) * first_full).astype(jnp.bfloat16)
    second_full = whole_conv(1, gated_cols)
    mixed_cols = (second_gate.astype(jnp.float32) * second_full).astype(jnp.bfloat16)
    gated, mixed_in = (
        lax.all_to_all(gated_cols, "ctx", split_axis=0, concat_axis=1, tiled=True),
        lax.all_to_all(mixed_cols, "ctx", split_axis=0, concat_axis=1, tiled=True),
    )
    partial_out = jnp.dot(mixed_in, w_out, preferred_element_type=jnp.float32)
    mixed = lax.psum_scatter(partial_out, "chan", scatter_dimension=1, tiled=True).astype(
        jnp.bfloat16
    )
    return (mixed, gated)


MESH = pl.DeviceIdType.MESH


def layer_kernel(
    n, cn, inputs, gain_hbm, w_in, w_out, history, filt_far, filt_near,
    fwd_hi_hbm, fwd_lo_hbm, inv_hi_hbm, inv_lo_hbm, out, gain, fwd_hi, fwd_lo, inv_hi, inv_lo, table_sem,
    x_all, normed, win, wout, h_stage, f_stage, h_all, f_all, near, wide, h_spec, f_spec,
    acc, fresh_out, fresh_all, back_out, g_all, m_all, m_full, part, part_all,
    x_local, x_send, x_recv, hs_sem, fs_sem, win_sem, wout_sem, near_sem,
    h_send, h_recv, f_send, f_recv, v_send, v_recv, g_send, g_recv, m_send, m_recv, p_send, p_recv,
):
    me = lax.axis_index("ctx")
    mine = lax.axis_index("chan")
    rows, width = inputs.shape
    block = history.shape[0]
    cols = width // n

    def lanes(d):
        return pl.ds(pl.multiple_of(d * cols, 128), cols)

    def remote(src, dst, send, recv, where):
        return pltpu.make_async_remote_copy(
            src_ref=src, dst_ref=dst, send_sem=send, recv_sem=recv,
            device_id=where, device_id_type=MESH,
        )

    def ctx_peer(s):
        return lax.rem(me + s, n)

    def chan_peer(s):
        return lax.rem(mine + s, cn)

    barrier = pltpu.get_barrier_semaphore()
    for s in range(1, n):
        pl.semaphore_signal(barrier, inc=1, device_id={"ctx": ctx_peer(s)}, device_id_type=MESH)
    for s in range(1, cn):
        pl.semaphore_signal(barrier, inc=1, device_id={"chan": chan_peer(s)}, device_id_type=MESH)

    x_copy = pltpu.make_async_copy(inputs, x_all.at[mine], x_local)
    x_copy.start()
    h_local, f_local = [], []
    for s in range(n):
        d = ctx_peer(s)
        h_to = h_all.at[me] if s == 0 else h_stage.at[s - 1]
        f_to = f_all.at[me] if s == 0 else f_stage.at[s - 1]
        h_local.append(pltpu.make_async_copy(history.at[:, :, lanes(d)], h_to, hs_sem.at[s]))
        f_local.append(pltpu.make_async_copy(filt_far.at[:, :, lanes(d)], f_to, fs_sem.at[s]))
    near_copy = pltpu.make_async_copy(filt_near.at[:, :, lanes(me)], near, near_sem)
    order = list(range(1, n)) + [0]
    for s in order:
        h_local[s].start()
        f_local[s].start()
    near_copy.start()
    table_copies = []
    for at, (source, table) in enumerate(
        [
            (fwd_hi_hbm, fwd_hi), (fwd_lo_hbm, fwd_lo), (gain_hbm, gain),
            (inv_hi_hbm, inv_hi), (inv_lo_hbm, inv_lo),
        ]
    ):
        copy = pltpu.make_async_copy(source, table, table_sem.at[at])
        copy.start()
        table_copies.append(copy)
    pl.semaphore_wait(barrier, n + cn - 2)

    x_copies = []
    for s in range(1, cn):
        copy = remote(
            inputs, x_all.at[mine], x_send.at[s], x_recv.at[s], {"chan": chan_peer(s)}
        )
        copy.start()
        x_copies.append(copy)
    h_copies, f_copies = [None] * n, [None] * n
    for s in order[:-1]:
        where = {"ctx": ctx_peer(s)}
        h_local[s].wait()
        h_copies[s] = remote(h_stage.at[s - 1], h_all.at[me], h_send.at[s], h_recv.at[s], where)
        h_copies[s].start()
        f_local[s].wait()
        f_copies[s] = remote(f_stage.at[s - 1], f_all.at[me], f_send.at[s], f_recv.at[s], where)
        f_copies[s].start()

    win_copies = []
    for i in range(3):
        for j in range(cn):
            copy = pltpu.make_async_copy(
                w_in.at[i, pl.ds(j * width, width)], win.at[i * cn + j], win_sem.at[i * cn + j]
            )
            copy.start()
            win_copies.append(copy)
    wout_copies = []
    for j in range(cn):
        copy = pltpu.make_async_copy(
            w_out.at[:, pl.ds(j * width, width)], wout.at[j], wout_sem.at[j]
        )
        copy.start()
        wout_copies.append(copy)

    def forward(x):
        return times(fwd_hi[...], x) + times(fwd_lo[...], x)

    def halves(ref):
        wide[...] = ref.reshape(2 * block, cols)[...].astype(jnp.float32)
        return [
            wide[pl.ds(c, block, stride=2), :].astype(jnp.bfloat16) for c in range(2)
        ]

    def transform(k):
        x = jnp.concatenate(halves(h_all.at[k]) + halves(f_all.at[k]), axis=1)
        spec = forward(x)
        h_spec[k] = spec[:, : 2 * cols]
        f_spec[k] = spec[:, 2 * cols :]

    h_local[0].wait()
    f_local[0].wait()
    near_copy.wait()
    for copy in table_copies:
        copy.wait()
    f_spec[n] = forward(jnp.concatenate(halves(near), axis=1))
    transform(me)

    x_copy.wait()
    for copy in x_copies:
        copy.wait_recv()
    square = jnp.zeros((rows, 1), jnp.float32)
    for j in range(cn):
        part_x = x_all[j].astype(jnp.float32)
        square = square + jnp.sum(part_x * part_x, axis=-1, keepdims=True)
    scale = lax.rsqrt(square / (cn * width) + 1e-06)
    for j in range(cn):
        normed[j] = (x_all[j].astype(jnp.float32) * scale * gain[:, j * width : (j + 1) * width]).astype(jnp.bfloat16)

    for i in range(3):
        for j in range(cn):
            win_copies[i * cn + j].wait()

        @pl.loop(0, n // 2 if n % 2 == 0 else n)
        def _(q):
            step = 2 if n % 2 == 0 else 1
            span = step * cols
            at = pl.ds(pl.multiple_of(q * span, 128), span)
            proj = times(normed[0], win[i * cn, :, at])
            for j in range(1, cn):
                proj = proj + times(normed[j], win[i * cn + j, :, at])
            for p in range(step):
                fresh_out[q * step + p, i] = proj[:, p * cols : (p + 1) * cols].astype(jnp.bfloat16)

    v_local = pltpu.make_async_copy(fresh_out.at[me], fresh_all.at[me], v_recv.at[0])
    v_local.start()
    v_copies = []
    for s in range(1, n):
        d = ctx_peer(s)
        copy = remote(
            fresh_out.at[d], fresh_all.at[me], v_send.at[s], v_recv.at[s], {"ctx": d}
        )
        copy.start()
        v_copies.append(copy)

    chunk = 32

    def add_term(k, first):
        @pl.loop(0, block // chunk)
        def _(r):
            low = pl.ds(pl.multiple_of(r * chunk, chunk), chunk)
            high = pl.ds(pl.multiple_of(block + r * chunk, chunk), chunk)
            odd = lax.broadcasted_iota(jnp.int32, (chunk, 2 * cols), 0) % 2
            turn = 1.0 - 2.0 * odd.astype(jnp.float32)
            win_re = f_spec[k, low, :] + turn * f_spec[k + 1, high, :]
            win_im = f_spec[k, high, :] - turn * f_spec[k + 1, low, :]
            old_re, old_im = h_spec[k, low, :], h_spec[k, high, :]
            sum_re = win_re * old_re + win_im * old_im
            sum_im = win_im * old_re - win_re * old_im
            if not first:
                sum_re = sum_re + acc[low, :]
                sum_im = sum_im + acc[high, :]
            acc[low, :] = sum_re
            acc[high, :] = sum_im

    def add_fresh(which, values):
        at = slice(which * cols, (which + 1) * cols)
        new = forward(values)
        new_re, new_im = new[:block], new[block:]
        near_re, near_im = f_spec[n, :block, at], f_spec[n, block:, at]
        acc[:block, at] += near_re * new_re + near_im * new_im
        acc[block:, at] += near_im * new_re - near_re * new_im

    fresh_rows = n * rows
    for s in range(1, n):
        if s == n - 1:
            v_local.wait()
            for copy in v_copies:
                copy.wait_recv()
            add_fresh(0, fresh_all[:, 0].reshape(fresh_rows, cols))
        h_copies[s].wait_recv()
        f_copies[s].wait_recv()
        k = lax.rem(me + n - s, n)
        transform(k)
        add_term(k, s == 1)
    add_term(me, False)

    def inverse(which):
        whole = acc[:, which * cols : (which + 1) * cols]
        high = whole.astype(jnp.bfloat16)
        low = (whole - high.astype(jnp.float32)).astype(jnp.bfloat16)
        both = times(inv_hi[...], jnp.concatenate([high, low], axis=1))
        return both[:, :cols] + both[:, cols:] + times(inv_lo[...], high)

    def send_back(index, every, send, recv):
        local = pltpu.make_async_copy(back_out.at[index, me], every.at[me], recv.at[0])
        local.start()
        copies = []
        for s in range(1, n):
            d = ctx_peer(s)
            copy = remote(
                back_out.at[index, d], every.at[me], send.at[s], recv.at[s], {"ctx": d}
            )
            copy.start()
            copies.append(copy)
        return local, copies

    first = inverse(0)
    gate_one = fresh_all[:, 1].reshape(fresh_rows, cols).astype(jnp.float32)
    gated_cols = (gate_one * first).astype(jnp.bfloat16)
    back_out[0] = gated_cols.reshape(n, rows, cols)
    g_local, g_copies = send_back(0, g_all, g_send, g_recv)
    add_fresh(1, gated_cols)
    second = inverse(1)
    gate_two = fresh_all[:, 2].reshape(fresh_rows, cols).astype(jnp.float32)
    back_out[1] = (gate_two * second).astype(jnp.bfloat16).reshape(n, rows, cols)
    m_local, m_copies = send_back(1, m_all, m_send, m_recv)

    g_local.wait()
    for copy in g_copies:
        copy.wait_recv()
    for j in range(n):
        out[1, :, j * cols : (j + 1) * cols] = g_all[j]
    for copy in wout_copies:
        copy.wait()
    m_local.wait()
    for copy in m_copies:
        copy.wait_recv()
    for j in range(n):
        m_full[:, j * cols : (j + 1) * cols] = m_all[j]
    p_copies = []
    half = cn // 2
    for s in [half] + [s for s in range(1, cn) if s != half] + [0]:
        d = chan_peer(s)
        product = times(m_full[...], wout[d])
        if s > 0:
            part[s] = product.astype(jnp.bfloat16)
            copy = remote(part.at[s], part_all.at[s], p_send.at[s], p_recv.at[s], {"chan": d})
            copy.start()
            p_copies.append((s, copy))
    result = product
    for s, copy in p_copies:
        copy.wait_recv()
        result = result + part_all[s].astype(jnp.float32)
    out[0] = result.astype(jnp.bfloat16)

    for copy in x_copies + h_copies[1:] + f_copies[1:] + v_copies + g_copies + m_copies + [c for _, c in p_copies]:
        copy.wait_send()


def fused_layer(inputs, gain, w_in, w_out, history, filt_far, filt_near):
    n, cn = lax.axis_size("ctx"), lax.axis_size("chan")
    rows, width = inputs.shape
    block = history.shape[0]
    cols = width // n
    (fwd_hi, fwd_lo), (inv_hi, inv_lo), _ = transforms(block)
    f32, bf16 = jnp.float32, jnp.bfloat16
    vmem = pl.BlockSpec(memory_space=pltpu.VMEM)
    anywhere = pl.BlockSpec(memory_space=pl.ANY)
    dma = pltpu.SemaphoreType.DMA
    both = pl.pallas_call(
        functools.partial(layer_kernel, n, cn),
        out_shape=jax.ShapeDtypeStruct((2, rows, width), bf16),
        in_specs=[anywhere] * 11,
        out_specs=vmem,
        scratch_shapes=[
            pltpu.VMEM((1, cn * width), f32),
            pltpu.VMEM(fwd_hi.shape, bf16),
            pltpu.VMEM(fwd_lo.shape, bf16),
            pltpu.VMEM(inv_hi.shape, bf16),
            pltpu.VMEM(inv_lo.shape, bf16),
            dma((5,)),
            pltpu.VMEM((cn, rows, width), bf16),
            pltpu.VMEM((cn, rows, width), bf16),
            pltpu.VMEM((3 * cn, width, width), bf16),
            pltpu.VMEM((cn, width, width), bf16),
            pltpu.VMEM((n - 1, block, 2, cols), bf16),
            pltpu.VMEM((n - 1, block, 2, cols), bf16),
            pltpu.VMEM((n, block, 2, cols), bf16),
            pltpu.VMEM((n, block, 2, cols), bf16),
            pltpu.VMEM((block, 2, cols), bf16),
            pltpu.VMEM((2 * block, cols), f32),
            pltpu.VMEM((n, 2 * block, 2 * cols), f32),
            pltpu.VMEM((n + 1, 2 * block, 2 * cols), f32),
            pltpu.VMEM((2 * block, 2 * cols), f32),
            pltpu.VMEM((n, 3, rows, cols), bf16),
            pltpu.VMEM((n, 3, rows, cols), bf16),
            pltpu.VMEM((2, n, rows, cols), bf16),
            pltpu.VMEM((n, rows, cols), bf16),
            pltpu.VMEM((n, rows, cols), bf16),
            pltpu.VMEM((rows, width), bf16),
            pltpu.VMEM((cn, rows, width), bf16),
            pltpu.VMEM((cn, rows, width), bf16),
            dma, dma((cn,)), dma((cn,)), dma((n,)), dma((n,)), dma((3 * cn,)), dma((cn,)), dma,
        ]
        + [dma((n,))] * 10
        + [dma((cn,))] * 2,
        compiler_params=pltpu.CompilerParams(
            collective_id=0, has_side_effects=True, vmem_limit_bytes=60 * 1024 * 1024
        ),
    )(
        inputs, gain.reshape(1, cn * width), w_in.transpose(1, 0, 2), w_out, history, filt_far,
        filt_near, fwd_hi, fwd_lo, inv_hi, inv_lo,
    )
    return both[0], both[1]


def per_device(inputs, gain, w_in, w_out, history, filt_far, filt_near):
    n = lax.axis_size("ctx")
    rows, width = inputs.shape
    fits = (
        width % (128 * n) == 0
        and rows % 16 == 0
        and history.shape[0] == filt_near.shape[0] == n * rows
    )
    layer = fused_layer if fits else plain_layer
    return layer(inputs, gain, w_in, w_out, history, filt_far, filt_near)


def solution(mesh):
    placed = (
        P("ctx", "chan"),
        P(),
        P(None, None, "chan"),
        P("chan", None),
        P("ctx", None, "chan"),
        P("ctx", None, "chan"),
        P(None, None, "chan"),
    )
    return jax.shard_map(
        per_device,
        mesh=mesh,
        in_specs=placed,
        out_specs=(P("ctx", "chan"), P("ctx", "chan")),
        check_vma=False,
    )
```
